32 devices in a mesh: row: 8 (over y, x, core), col: 4 (over z).
Axes of the slice: x: 2, y: 2, z: 4, core: 2. Of those that a mesh axis runs over, the one named last changes fastest.
Arguments:
- positions: float32 [3, 32768], P(None, ('row', 'col')), may hold values from 0 to 1
- segments: float32 [3, 32768], P(None, ('row', 'col')), may hold values from -1.2 to 1.2
- radius: float32 [32768], P(('row', 'col')), may hold values from 0.05 to 0.2
- currents: float32 [2, 32768], P(None, ('row', 'col')), may hold values from -6 to 6
- resist: float32 [32768], P(('row', 'col')), may hold values from 0.3 to 3
- slot_of: int32 [32768], P(('row', 'col')), may hold values from 0 to 1023, as said below
- pair_list: int32 [1024, 2], P(('row', 'col')), may hold values from 0 to 63, as said below
- near_flag: int32 [1024], P(('row', 'col')), may hold values from 0 to 2, as said below
Outputs:
- voltage: float32 [2, 32768], P(None, ('row', 'col'))
The draws below stay inside these ranges and needn't reach their ends.
Inputs may be any that keep to these rules, and one draw needn't show every extreme that they name: `slot_of`: the elements of shard d hold the values 0 to 1023 once each; a value s puts the element in cluster d * 2 + s // 512. `pair_list`: shard d = r * 4 + c lists 32 slots; each live slot holds a pair (I, J) with I <= J, I in clusters r * 2 * 4 to (r + 1) * 2 * 4 - 1 and (J // 2) % 4 = c; a pair stands in one live slot at most, over all shards. Empty slots hold I = r * 2 * 4 and J = c * 2. `near_flag`: 0 marks an empty slot.
All inputs are finite; a program needn't handle non-finite values.
Results may differ from the reference program's by a relative error of at most 0.0003.
Values sent between devices are 32-bit elements; how exact they have to be, the bound alone decides.
A program may use at most 64 MiB of HBM per device.

```python
import math
import jax
import jax.numpy as jnp
from jax import lax

CS = 512
CPD = 2
PCAP = 32
NE = 32768
N_ROW = 8
N_COL = 4
DEVICES = 32


def list_layout(key):
    base_key = jax.random.fold_in(key, 7177)
    row_span = CPD * N_COL
    col_span = CPD * N_ROW
    square = row_span * col_span
    device_keys = jax.random.split(base_key, DEVICES)

    def one_device(device_id, device_key):
        row_pos = device_id // N_COL
        col_pos = device_id % N_COL
        candidate = jnp.arange(square, dtype=jnp.int32)
        first_local = candidate // col_span
        second_local = candidate % col_span
        first_id = row_pos * row_span + first_local
        second_id = (second_local // CPD * N_COL + col_pos) * CPD + second_local % CPD
        allowed = second_id >= first_id
        allowed_count = jnp.sum(allowed.astype(jnp.int32))
        key_order, key_jitter, key_near, key_shuffle = jax.random.split(device_key, 4)
        priority = jax.random.permutation(key_order, square).astype(jnp.int32)
        scores = jnp.where(allowed, priority + square, priority)
        _, chosen = lax.top_k(scores, PCAP)
        jitter = jax.random.randint(key_jitter, (), 0, PCAP // 4 + 1)
        wanted = PCAP * (N_ROW - row_pos) // N_ROW - jnp.where(row_pos > 0, jitter, 0)
        live_count = jnp.minimum(allowed_count, jnp.maximum(wanted, 1))
        slot_index = jnp.arange(PCAP, dtype=jnp.int32)
        is_live = slot_index < live_count
        pick_first = jnp.where(is_live, first_id[chosen], row_pos * row_span)
        pick_second = jnp.where(is_live, second_id[chosen], col_pos * CPD)
        near_roll = jax.random.randint(key_near, (PCAP,), 0, 8)
        is_close = pick_second - pick_first < 2 * row_span
        is_near = jnp.where(is_close, near_roll < 4, near_roll < 1)
        flags = jnp.where(is_live, jnp.where(is_near, 2, 1), 0).astype(jnp.int32)
        shuffle = jax.random.permutation(key_shuffle, PCAP)
        pairs = jnp.stack([pick_first, pick_second], 1).astype(jnp.int32)
        return (pairs[shuffle], flags[shuffle])
    pairs, flags = jax.vmap(one_device)(jnp.arange(DEVICES, dtype=jnp.int32), device_keys)
    return (pairs.reshape(DEVICES * PCAP, 2), flags.reshape(DEVICES * PCAP))


def draw_pair_list(key, part):
    pairs, _ = list_layout(key)
    return pairs


def draw_near_flag(key, part):
    _, flags = list_layout(key)
    return flags


def draw_slot_of(key, part):
    per_device = CPD * CS
    device_keys = jax.random.split(jax.random.fold_in(key, 3301), DEVICES)

    def one_device(device_key):
        return jax.random.permutation(device_key, per_device)
    return jax.vmap(one_device)(device_keys).reshape(-1).astype(jnp.int32)


def level_of(stream_key, extent, shards, smallest, top_value):
    def one(dim, shards_of):
        steps = jax.random.uniform(jax.random.fold_in(jax.random.fold_in(stream_key, 6), dim), (shards_of,), jnp.float32, smallest / len(shards), top_value / len(shards))
        return jnp.repeat(jnp.exp(steps), extent[dim] // shards_of).reshape((-1,) + (1,) * (len(extent) - dim - 1))

    factor_of = one(*shards[0])
    for cut in shards[1:]:
        factor_of = factor_of * one(*cut)
    return factor_of


def noise(stream_key, extent, scale, limit, shards=(), kind=jnp.bfloat16):
    gain = level_of(stream_key, extent, shards, -0.22, 0.18) if shards else 1.0
    values = jax.random.normal(stream_key, extent, jnp.float32) * scale * gain
    return jnp.minimum(jnp.maximum(values, -limit), limit).astype(kind)


def setup_inputs(seed: int = 0) -> dict:
    arg_keys = jax.random.split(jax.random.key(seed), 9)
    positions = jnp.clip(1.0 * jax.random.uniform(arg_keys[0], (3, NE), jnp.float32) ** level_of(arg_keys[0], (3, NE), ((1, 32),), -0.2, 0.2), 0.0, 1.0)
    segments = noise(arg_keys[1], (3, NE), 0.2, 1.2, ((1, 32),), jnp.float32)
    radius = jnp.clip(jnp.exp(math.log(0.2) - 1.3862944 * jax.random.uniform(arg_keys[2], (NE,), jnp.float32) ** level_of(arg_keys[2], (NE,), ((0, 32),), -0.2, 0.2)), 0.05, 0.2)
    currents = noise(arg_keys[3], (2, NE), 1.0, 6.0, ((1, 32),), jnp.float32)
    resist = jnp.clip(jnp.exp(math.log(3.0) - 2.3025851 * jax.random.uniform(arg_keys[4], (NE,), jnp.float32) ** level_of(arg_keys[4], (NE,), ((0, 32),), -0.2, 0.2)), 0.3, 3.0)
    slot_of = draw_slot_of(jax.random.fold_in(arg_keys[8], 71), 0)
    pair_list = draw_pair_list(jax.random.fold_in(arg_keys[8], 71), 0)
    near_flag = draw_near_flag(jax.random.fold_in(arg_keys[8], 71), 0)
    return dict(positions=positions, segments=segments, radius=radius, currents=currents, resist=resist, slot_of=slot_of, pair_list=pair_list, near_flag=near_flag)


gauss_step = 0.5 / math.sqrt(3.0)
kernel_gain = 0.25

def tile_block(points_first, vectors_first, radii_first, points_second, vectors_second, radii_second, is_near):
    softening = radii_first[:, None] ** 2 + radii_second[None, :] ** 2
    alignment = vectors_first[0][:, None] * vectors_second[0][None, :]
    for component in (1, 2):
        alignment = alignment + vectors_first[component][:, None] * vectors_second[component][None, :]

    def far_part():
        squared = softening
        for component in range(3):
            squared = squared + (points_first[component][:, None] - points_second[component][None, :]) ** 2
        return 1.0 / jnp.sqrt(squared)

    def near_part():
        summed = jnp.zeros_like(softening)
        for sign_first in (-1.0, 1.0):
            for sign_second in (-1.0, 1.0):
                squared = softening
                for component in range(3):
                    moved_first = points_first[component] + sign_first * gauss_step * vectors_first[component]
                    moved_second = points_second[component] + sign_second * gauss_step * vectors_second[component]
                    squared = squared + (moved_first[:, None] - moved_second[None, :]) ** 2
                summed = summed + 1.0 / jnp.sqrt(squared)
        return 0.25 * summed
    inverse = lax.cond(is_near, near_part, far_part)
    return kernel_gain * alignment * inverse

def reference(positions, segments, radius, currents, resist, slot_of, pair_list, near_flag):
    per_device = CPD * CS
    device_of = jnp.arange(NE, dtype=jnp.int32) // per_device
    global_slot = (device_of * per_device + slot_of).astype(jnp.int32)
    packed = jnp.concatenate([positions, segments, radius[None, :], currents], 0)
    ordered = jnp.zeros_like(packed).at[:, global_slot].set(packed)

    def advance(induced_sum, slot_entry):
        pair_entry, flag_value = slot_entry
        first_id = pair_entry[0].astype(jnp.int32)
        second_id = pair_entry[1].astype(jnp.int32)
        block_first = lax.dynamic_slice_in_dim(ordered, first_id * CS, CS, 1)
        block_second = lax.dynamic_slice_in_dim(ordered, second_id * CS, CS, 1)
        kernel_tile = tile_block(block_first[0:3], block_first[3:6], block_first[6], block_second[0:3], block_second[3:6], block_second[6], flag_value == 2)
        weight_live = (flag_value > 0).astype(induced_sum.dtype)
        weight_mirror = weight_live * (first_id != second_id).astype(induced_sum.dtype)
        direct_part = weight_live * jnp.dot(block_second[7:9], kernel_tile.T, precision=lax.Precision.HIGHEST)
        mirror_part = weight_mirror * jnp.dot(block_first[7:9], kernel_tile, precision=lax.Precision.HIGHEST)
        current = lax.dynamic_slice_in_dim(induced_sum, first_id * CS, CS, 1)
        induced_sum = lax.dynamic_update_slice_in_dim(induced_sum, current + direct_part, first_id * CS, 1)
        current = lax.dynamic_slice_in_dim(induced_sum, second_id * CS, CS, 1)
        induced_sum = lax.dynamic_update_slice_in_dim(induced_sum, current + mirror_part, second_id * CS, 1)
        return (induced_sum, None)
    start_sum = jnp.zeros((2, NE), packed.dtype)
    induced_field, _ = lax.scan(advance, start_sum, (pair_list, near_flag))
    induced = induced_field[:, global_slot]
    voltage_real = resist * currents[0] - induced[1]
    voltage_imag = resist * currents[1] + induced[0]
    return jnp.stack([voltage_real, voltage_imag])
```

```python
import functools
import math

import jax
import jax.numpy as jnp
from jax import lax
from jax.experimental import pallas as pl
from jax.experimental.pallas import tpu as pltpu
from jax.sharding import PartitionSpec as P

CS = 512
F32 = jnp.float32
BF16 = jnp.bfloat16
MESH = pl.DeviceIdType.MESH
gauss_step = 0.5 / math.sqrt(3.0)
kernel_gain = 0.25
VMEM = pl.BlockSpec(memory_space=pltpu.VMEM)
TALL = 256
STEP = 128
FAR = 2


def split_three(value):
    high = value.astype(BF16).astype(F32)
    rest = value - high
    middle = rest.astype(BF16).astype(F32)
    return high, middle, rest - middle


def dot_nn(left, right):
    return lax.dot_general(left, right, (((1,), (0,)), ((), ())), preferred_element_type=F32)


def dot_nt(left, right):
    return lax.dot_general(left, right, (((1,), (1,)), ((), ())), preferred_element_type=F32)


def one_hot_rows(slots, start, count):
    rows = lax.broadcasted_iota(jnp.int32, (count, slots.shape[1]), 0) + start
    return jnp.where(rows == slots, 1.0, 0.0).astype(BF16)


def order_into(pos, seg, rad, cur, slot, pair, flag, main, extra, stack):
    clusters = main.shape[0]
    slots = slot[...]
    stack[...] = jnp.zeros_like(stack)
    for source, row in ((pos, 0), (seg, 3), (rad, 6), (cur, 7)):
        count = source.shape[0]
        for part, piece in enumerate(split_three(source[...])):
            stack[part * 16 + row : part * 16 + row + count, :] = piece
    parts = stack[...].astype(BF16)
    for cluster in range(clusters):
        sums = dot_nt(parts, one_hot_rows(slots, cluster * CS, CS))
        ordered = sums[0:16] + sums[16:32] + sums[32:48]
        main[cluster] = ordered[0:8]
        extra[cluster : cluster + 1, :] = ordered[8:9]
    listed = pair.shape[1]
    extra[clusters : clusters + 2, :] = jnp.zeros((2, CS), F32)
    extra[clusters : clusters + 1, 0:listed] = pair[0:1, :].astype(F32)
    extra[clusters : clusters + 1, 128 : 128 + listed] = pair[1:2, :].astype(F32)
    extra[clusters : clusters + 1, 256 : 256 + listed] = flag[...].astype(F32)


def tile_rows(count):
    return lax.broadcasted_iota(jnp.int32, (8, count), 0)


def pair_kernel(
    main, extra, resist, cur, slot, out,
    acc, left, right, weight, retired, inverse, stack,
):
    devices, clusters = main.shape[0], main.shape[1]
    local = cur.shape[1]
    me = lax.axis_index("row") * lax.axis_size("col") + lax.axis_index("col")
    acc[...] = jnp.zeros_like(acc)
    retired[...] = jnp.zeros_like(retired)
    inverse[...] = jnp.zeros_like(inverse)
    rows = tile_rows(CS)

    lists = extra[:, clusters, :]
    first_ids, second_ids, flags = lists[:, 0:128], lists[:, 128:256], lists[:, 256:384]
    near_masks, far_masks, codes = [], [], []
    for k in range(clusters):
        own = (me * clusters + k).astype(F32)
        is_first = first_ids == own
        match = jnp.where(is_first | (second_ids == own), flags, 0.0)
        near_masks.append(jnp.where(match > 1.5, 1.0, 0.0))
        far_masks.append(jnp.where((match > 0.5) & (match < 1.5), 1.0, 0.0))
        codes.append(jnp.where(is_first, second_ids, first_ids) + 4096.0 * k)
    masks = jnp.concatenate(near_masks + far_masks, 0)
    code = jnp.concatenate(codes + codes, 0)
    marks = masks.astype(BF16)
    entries = masks.shape[0]
    before_lane = jnp.where(
        lax.broadcasted_iota(jnp.int32, (128, 128), 0) < lax.broadcasted_iota(jnp.int32, (128, 128), 1),
        1.0,
        0.0,
    ).astype(BF16)
    before_row = jnp.where(
        lax.broadcasted_iota(jnp.int32, (entries, entries), 1)
        < lax.broadcasted_iota(jnp.int32, (entries, entries), 0),
        1.0,
        0.0,
    ).astype(BF16)
    in_row = dot_nn(marks, jnp.ones((128, 128), BF16)).astype(BF16)
    rank = jnp.where(
        masks > 0.5, dot_nn(marks, before_lane) + dot_nn(before_row, in_row), -1.0
    ).astype(jnp.int32)
    near_count = jnp.sum(masks[0 : clusters * devices]).astype(jnp.int32)
    count = jnp.sum(masks).astype(jnp.int32)

    def pick(turn):
        return jnp.sum(jnp.where(rank == turn, code, 0.0)).astype(jnp.int32)

    def moved(block, turned, sign):
        points = block - 0.5
        if sign:
            points = points + (sign * gauss_step) * turned
        squares = jnp.where(rows < 3, points * points, jnp.where(rows == 3, turned * turned, 0.0))
        return points, jnp.sum(squares, axis=0, keepdims=True)

    def stacked(value, order):
        parts = split_three(value)
        return [
            jnp.concatenate([parts[order[n]], parts[order[n + 1]]], 0) for n in range(0, 6, 2)
        ]

    def left_side(block, turned, sign):
        points, norm = moved(block, turned, sign)
        value = jnp.where(rows < 3, points, jnp.where(rows == 3, norm, jnp.where(rows == 4, 1.0, 0.0)))
        return jnp.concatenate(stacked(value, (0, 0, 1, 1, 0, 2)), 0)

    def right_side(block, turned, sign):
        points, norm = moved(block, turned, sign)
        value = jnp.where(
            rows < 3, -2.0 * points, jnp.where(rows == 3, 1.0, jnp.where(rows == 4, norm, 0.0))
        )
        return stacked(value, (0, 1, 0, 1, 2, 0))

    def prepare(unit, now, scale, signs):
        cluster = now % 4096
        device, place = cluster // clusters, cluster % clusters
        block = main[device, place]
        imag = extra[device, pl.ds(place, 1), :]
        turned = pltpu.roll(block, 5, 0)
        for index, sign in enumerate(signs):
            for part, piece in enumerate(right_side(block, turned, sign)):
                right[unit, index, 16 * part : 16 * part + 16, :] = piece.astype(BF16)
        value = jnp.where(rows < 3, turned * block[7:8], jnp.where(rows < 6, block * imag, 0.0))
        value = value * scale
        high = value.astype(BF16).astype(F32)
        weight[unit] = jnp.concatenate([high, value - high], 0).astype(BF16)

    def retire(unit, k):
        weights = retired[unit]
        weights = jnp.concatenate([weights, weights], 1)
        for start in range(0, CS, TALL):
            term = dot_nt(weights, inverse[unit, start : start + TALL, :])
            acc[k, :, start : start + TALL] += term

    def compute(unit, k, lefts, count_right):
        sides = [right[unit, index] for index in range(count_right)]
        for start in range(0, CS, STEP):
            total = 0.0
            for variant in lefts:
                one = left[k, variant, start : start + STEP, :]
                for other in sides:
                    total = total + lax.rsqrt(dot_nn(one, other))
            high = total.astype(BF16)
            inverse[unit, start : start + STEP, 0:CS] = high
            inverse[unit, start : start + STEP, CS:] = (total - high.astype(F32)).astype(BF16)
        retired[unit] = weight[unit]

    for k in range(clusters):
        block = main[me, k]
        turned = pltpu.roll(block, 5, 0)
        for variant, sign in enumerate((0, -1, 1)):
            left[k, variant] = left_side(block, turned, sign).T.astype(BF16)

    near_gain, far_gain = kernel_gain * 0.25, kernel_gain

    def visit_near(turn, state):
        now, later, last = state
        retire(0, last)
        k = now // 4096
        compute(0, k, (1, 2), 2)
        prepare(0, later, near_gain, (-1, 1))
        return later, pick(turn + 2), k

    def far_scale(turn):
        return jnp.where(turn < count, far_gain, 0.0)

    def visit_far(step, state):
        turn = near_count + FAR * step
        nows, laters, lasts = state
        for unit in range(FAR):
            retire(unit, lasts[unit])
        ks = tuple(nows[unit] // 4096 for unit in range(FAR))
        for unit in range(FAR):
            compute(unit, ks[unit], (0,), 1)
        for unit in range(FAR):
            prepare(unit, laters[unit], far_scale(turn + FAR + unit), (0,))
        return laters, tuple(pick(turn + 2 * FAR + unit) for unit in range(FAR)), ks

    begin = pick(0)
    prepare(0, begin, near_gain, (-1, 1))
    _, _, last = lax.fori_loop(0, near_count, visit_near, (begin, pick(1), 0))
    nows = tuple(pick(near_count + unit) for unit in range(FAR))
    laters = tuple(pick(near_count + FAR + unit) for unit in range(FAR))
    for unit in range(FAR):
        prepare(unit, nows[unit], far_scale(near_count + unit), (0,))
    _, _, lasts = lax.fori_loop(
        0,
        (count - near_count + FAR - 1) // FAR,
        visit_far,
        (nows, laters, (last,) + (0,) * (FAR - 1)),
    )
    for unit in range(FAR):
        retire(unit, lasts[unit])

    tiles = CS // 128
    for k in range(clusters):
        both = acc[k, 0:8, :] + acc[k, 8:16, :]
        block = main[me, k]
        turned = pltpu.roll(block, 5, 0)
        real = jnp.sum(jnp.where(rows < 3, both * turned, 0.0), axis=0, keepdims=True)
        imag = jnp.sum(
            jnp.where((rows > 2) & (rows < 6), both * block, 0.0), axis=0, keepdims=True
        )
        for row, value in enumerate((real, imag)):
            for part, piece in enumerate(split_three(value)):
                for tile in range(tiles):
                    base = (part * 2 + row) * clusters * tiles + k * tiles + tile
                    stack[base : base + 1, :] = piece[:, 128 * tile : 128 * tile + 128]
    slots = slot[...]
    lanes = lax.rem(slots, 128)
    chosen = jnp.where(
        lax.broadcasted_iota(jnp.int32, (128, local), 0) == lanes, 1.0, 0.0
    ).astype(BF16)
    spread = dot_nn(stack[...].astype(BF16), chosen)
    height = clusters * tiles
    mine = lax.broadcasted_iota(jnp.int32, (height, local), 0) == slots // 128
    induced = []
    for row in range(2):
        whole = 0.0
        for part in range(3):
            base = (part * 2 + row) * height
            whole = whole + spread[base : base + height]
        induced.append(jnp.sum(jnp.where(mine, whole, 0.0), axis=0, keepdims=True))
    scaled = resist[...] * cur[...]
    out[0:1, :] = scaled[0:1] - induced[1]
    out[1:2, :] = scaled[1:2] + induced[0]


def pair_terms(main, extra, resist, currents, slot_of):
    clusters = main.shape[1]
    return pl.pallas_call(
        pair_kernel,
        out_shape=jax.ShapeDtypeStruct(currents.shape, F32),
        in_specs=[VMEM] * 5,
        out_specs=VMEM,
        scratch_shapes=[
            pltpu.VMEM((clusters, 16, CS), F32),
            pltpu.VMEM((clusters, 3, CS, 48), BF16),
            pltpu.VMEM((FAR, 2, 48, CS), BF16),
            pltpu.VMEM((FAR, 16, CS), BF16),
            pltpu.VMEM((FAR, 16, CS), BF16),
            pltpu.VMEM((FAR, CS, 2 * CS), BF16),
            pltpu.VMEM((6 * clusters * CS // 128, 128), F32),
        ],
    )(main, extra, resist[None, :], currents, slot_of[None, :])


def gather_kernel(
    pos, seg, rad, cur, slot, pair, flag, main_all, extra_all, stack, send_sem, recv_sem
):
    row_count, col_count = lax.axis_size("row"), lax.axis_size("col")
    row, col = lax.axis_index("row"), lax.axis_index("col")
    me = row * col_count + col
    chips = row_count // 2
    other = row + 1 - 2 * lax.rem(row, 2)
    gathered = (main_all, extra_all)

    def row_at(base, step):
        return lax.rem(base + 2 * step, row_count)

    def col_at(step):
        return lax.rem(col + step, col_count)

    barrier = pltpu.get_barrier_semaphore()
    peers = [(row, col_at(k)) for k in range(1, col_count)]
    peers += [(row_at(row, k), col) for k in range(1, chips)] + [(other, col)]
    for to_row, to_col in peers:
        pl.semaphore_signal(
            barrier, inc=1, device_id={"row": to_row, "col": to_col}, device_id_type=MESH
        )
    order_into(
        pos, seg, rad, cur, slot, pair, flag, main_all.at[me], extra_all.at[me], stack
    )
    pl.semaphore_wait(barrier, len(peers))

    def copies(origin, lane, to_row, to_col):
        return [
            pltpu.make_async_remote_copy(
                src_ref=target.at[origin],
                dst_ref=target.at[origin],
                send_sem=send_sem.at[part, lane],
                recv_sem=recv_sem.at[part, origin],
                device_id={"row": to_row, "col": to_col},
                device_id_type=MESH,
            )
            for part, target in enumerate(gathered)
        ]

    sent = []

    def push(origin, to_row, to_col):
        started = copies(origin, len(sent), to_row, to_col)
        for copy in started:
            copy.start()
        sent.append(started)

    def arrive(origin):
        for copy in copies(origin, 0, other, col):
            copy.wait_recv()

    def fan_out(origin):
        for k in range(1, chips):
            push(origin, row_at(row, k), col)
        push(origin, other, col)

    for k in range(1, col_count):
        push(me, row, col_at(k))
    fan_out(me)
    for k in range(1, col_count):
        origin = row * col_count + col_at(col_count - k)
        arrive(origin)
        fan_out(origin)
    for block in range(col_count):
        for k in range(1, chips):
            origin = row_at(row, chips - k) * col_count + col_at(col_count - block)
            arrive(origin)
            push(origin, other, col)
    for block in range(col_count):
        for k in range(chips):
            arrive(row_at(other, chips - k) * col_count + col_at(col_count - block))
    for started in sent:
        for copy in started:
            copy.wait_send()


def gather_all(positions, segments, radius, currents, slot_of, pair_list, near_flag):
    row_count, col_count = lax.axis_size("row"), lax.axis_size("col")
    devices = row_count * col_count
    local = positions.shape[1]
    clusters = local // CS
    lanes = col_count - 1 + col_count * (row_count - 1)
    return pl.pallas_call(
        gather_kernel,
        out_shape=(
            jax.ShapeDtypeStruct((devices, clusters, 8, CS), F32),
            jax.ShapeDtypeStruct((devices, clusters + 2, CS), F32),
        ),
        in_specs=[VMEM] * 7,
        out_specs=(VMEM, VMEM),
        scratch_shapes=[
            pltpu.VMEM((48, local), F32),
            pltpu.SemaphoreType.DMA((2, lanes)),
            pltpu.SemaphoreType.DMA((2, devices)),
        ],
        compiler_params=pltpu.CompilerParams(collective_id=0, has_side_effects=True),
    )(
        positions,
        segments,
        radius[None, :],
        currents,
        slot_of[None, :],
        pair_list.T,
        near_flag[None, :],
    )


def on_device(positions, segments, radius, currents, resist, slot_of, pair_list, near_flag):
    main_all, extra_all = gather_all(
        positions, segments, radius, currents, slot_of, pair_list, near_flag
    )
    return pair_terms(main_all, extra_all, resist, currents, slot_of)


def solution(mesh):
    return jax.shard_map(
        on_device,
        mesh=mesh,
        in_specs=(
            P(None, ("row", "col")),
            P(None, ("row", "col")),
            P(("row", "col")),
            P(None, ("row", "col")),
            P(("row", "col")),
            P(("row", "col")),
            P(("row", "col"), None),
            P(("row", "col")),
        ),
        out_specs=P(None, ("row", "col")),
        check_vma=False,
    )
```

```python
import functools
import math

import jax
import jax.numpy as jnp
from jax import lax
from jax.experimental import pallas as pl
from jax.experimental.pallas import tpu as pltpu
from jax.sharding import PartitionSpec as P

CS = 512
F32 = jnp.float32
BF16 = jnp.bfloat16
MESH = pl.DeviceIdType.MESH
gauss_step = 0.5 / math.sqrt(3.0)
kernel_gain = 0.25
VMEM = pl.BlockSpec(memory_space=pltpu.VMEM)
WIDE = 256
STEP = 128
FAR = 2


def split_three(value):
    high = value.astype(BF16).astype(F32)
    rest = value - high
    middle = rest.astype(BF16).astype(F32)
    return high, middle, rest - middle


def dot_nn(left, right):
    return lax.dot_general(left, right, (((1,), (0,)), ((), ())), preferred_element_type=F32)


def dot_nt(left, right):
    return lax.dot_general(left, right, (((1,), (1,)), ((), ())), preferred_element_type=F32)


def one_hot_rows(slots, start, count):
    rows = lax.broadcasted_iota(jnp.int32, (count, slots.shape[1]), 0) + start
    return jnp.where(rows == slots, 1.0, 0.0).astype(BF16)


def order_into(pos, seg, rad, cur, slot, pair, flag, main, extra, stack):
    clusters = main.shape[0]
    slots = slot[...]
    stack[...] = jnp.zeros_like(stack)
    for source, row in ((pos, 0), (seg, 3), (rad, 6), (cur, 7)):
        count = source.shape[0]
        for part, piece in enumerate(split_three(source[...])):
            stack[part * 16 + row : part * 16 + row + count, :] = piece
    parts = stack[...].astype(BF16)
    for cluster in range(clusters):
        sums = dot_nt(parts, one_hot_rows(slots, cluster * CS, CS))
        ordered = sums[0:16] + sums[16:32] + sums[32:48]
        main[cluster] = ordered[0:8]
        extra[cluster : cluster + 1, :] = ordered[8:9]
    listed = pair.shape[1]
    extra[clusters : clusters + 2, :] = jnp.zeros((2, CS), F32)
    extra[clusters : clusters + 1, 0:listed] = pair[0:1, :].astype(F32)
    extra[clusters : clusters + 1, 128 : 128 + listed] = pair[1:2, :].astype(F32)
    extra[clusters : clusters + 1, 256 : 256 + listed] = flag[...].astype(F32)


def tile_rows(count):
    return lax.broadcasted_iota(jnp.int32, (8, count), 0)


def pair_kernel(
    main, extra, resist, cur, slot, out,
    acc, target, source, weight, retired, inverse, stack,
):
    devices, clusters = main.shape[0], main.shape[1]
    local = cur.shape[1]
    me = lax.axis_index("row") * lax.axis_size("col") + lax.axis_index("col")
    acc[...] = jnp.zeros_like(acc)
    rows = tile_rows(CS)

    lists = extra[:, clusters, :]
    first_ids, second_ids, flags = lists[:, 0:128], lists[:, 128:256], lists[:, 256:384]
    near_masks, far_masks, codes = [], [], []
    for k in range(clusters):
        own = (me * clusters + k).astype(F32)
        is_first = first_ids == own
        match = jnp.where(is_first | (second_ids == own), flags, 0.0)
        near_masks.append(jnp.where(match > 1.5, 1.0, 0.0))
        far_masks.append(jnp.where((match > 0.5) & (match < 1.5), 1.0, 0.0))
        codes.append(jnp.where(is_first, second_ids, first_ids) + 4096.0 * k)
    masks = jnp.concatenate(near_masks + far_masks, 0)
    code = jnp.concatenate(codes + codes, 0)
    marks = masks.astype(BF16)
    entries = masks.shape[0]
    before_lane = jnp.where(
        lax.broadcasted_iota(jnp.int32, (128, 128), 0) < lax.broadcasted_iota(jnp.int32, (128, 128), 1),
        1.0,
        0.0,
    ).astype(BF16)
    before_row = jnp.where(
        lax.broadcasted_iota(jnp.int32, (entries, entries), 1)
        < lax.broadcasted_iota(jnp.int32, (entries, entries), 0),
        1.0,
        0.0,
    ).astype(BF16)
    in_row = dot_nn(marks, jnp.ones((128, 128), BF16)).astype(BF16)
    rank = jnp.where(
        masks > 0.5, dot_nn(marks, before_lane) + dot_nn(before_row, in_row), -1.0
    ).astype(jnp.int32)
    near_count = jnp.sum(masks[0 : clusters * devices]).astype(jnp.int32)
    count = jnp.sum(masks).astype(jnp.int32)

    def pick(turn):
        return jnp.sum(jnp.where(rank == turn, code, 0.0)).astype(jnp.int32)

    def moved(block, turned, sign):
        points = block - 0.5
        if sign:
            points = points + (sign * gauss_step) * turned
        squares = jnp.where(rows < 3, points * points, jnp.where(rows == 3, turned * turned, 0.0))
        return points, jnp.sum(squares, axis=0, keepdims=True)

    def stacked(value, order):
        parts = split_three(value)
        return [
            jnp.concatenate([parts[order[n]], parts[order[n + 1]]], 0) for n in range(0, 6, 2)
        ]

    def source_side(points, norm):
        value = jnp.where(
            rows < 3, -2.0 * points, jnp.where(rows == 3, 1.0, jnp.where(rows == 4, norm, 0.0))
        )
        return jnp.concatenate(stacked(value, (0, 1, 0, 1, 2, 0)), 0)

    def target_side(points, norm):
        value = jnp.where(rows < 3, points, jnp.where(rows == 3, norm, jnp.where(rows == 4, 1.0, 0.0)))
        return jnp.concatenate(stacked(value, (0, 0, 1, 1, 0, 2)), 0)

    def prepare(unit, now, scale, signs):
        cluster = now % 4096
        device, place = cluster // clusters, cluster % clusters
        block = main[device, place]
        imag = extra[device, pl.ds(place, 1), :]
        turned = pltpu.roll(block, 5, 0)
        for index, sign in enumerate(signs):
            side = source_side(*moved(block, turned, sign))
            source[unit, index] = side.T.astype(BF16)
        value = jnp.where(rows < 3, turned * block[7:8], jnp.where(rows < 6, block * imag, 0.0))
        value = value * scale
        high = value.astype(BF16).astype(F32)
        weight[unit] = jnp.concatenate([high, value - high], 0).astype(BF16)

    def retire(unit, k, start, across):
        weights = retired[unit, :, start : start + STEP]
        term = dot_nn(
            jnp.concatenate([weights, weights], 1),
            inverse[unit, start // STEP, :, across : across + WIDE],
        )
        place = jnp.maximum(k, 0)
        acc[place, :, across : across + WIDE] += jnp.where(k >= 0, term, 0.0)

    def compute(unit, k, last, targets, sources):
        sides = [target[k, index] for index in targets]
        for across in range(0, CS, WIDE):
            for start in range(0, CS, STEP):
                retire(unit, last, start, across)
                total = 0.0
                for index in range(sources):
                    one = source[unit, index, start : start + STEP, :]
                    for side in sides:
                        total = total + lax.rsqrt(dot_nn(one, side[:, across : across + WIDE]))
                high = total.astype(BF16)
                low = (total - high.astype(F32)).astype(BF16)
                inverse[unit, start // STEP, 0:STEP, across : across + WIDE] = high
                inverse[unit, start // STEP, STEP:, across : across + WIDE] = low
        retired[unit] = weight[unit]

    for k in range(clusters):
        block = main[me, k]
        turned = pltpu.roll(block, 5, 0)
        for index, sign in enumerate((0, -1, 1)):
            target[k, index] = target_side(*moved(block, turned, sign)).astype(BF16)

    near_gain, far_gain = kernel_gain * 0.25, kernel_gain

    def visit_near(turn, state):
        now, later, last = state
        k = now // 4096
        compute(0, k, last, (1, 2), 2)
        prepare(0, later, near_gain, (-1, 1))
        return later, pick(turn + 2), k

    def far_scale(turn):
        return jnp.where(turn < count, far_gain, 0.0)

    def visit_far(step, state):
        turn = near_count + FAR * step
        nows, laters, lasts = state
        ks = tuple(nows[unit] // 4096 for unit in range(FAR))
        for unit in range(FAR):
            compute(unit, ks[unit], lasts[unit], (0,), 1)
        for unit in range(FAR):
            prepare(unit, laters[unit], far_scale(turn + FAR + unit), (0,))
        return laters, tuple(pick(turn + 2 * FAR + unit) for unit in range(FAR)), ks

    begin = pick(0)
    prepare(0, begin, near_gain, (-1, 1))
    _, _, last = lax.fori_loop(0, near_count, visit_near, (begin, pick(1), -1))
    nows = tuple(pick(near_count + unit) for unit in range(FAR))
    laters = tuple(pick(near_count + FAR + unit) for unit in range(FAR))
    for unit in range(FAR):
        prepare(unit, nows[unit], far_scale(near_count + unit), (0,))
    _, _, lasts = lax.fori_loop(
        0,
        (count - near_count + FAR - 1) // FAR,
        visit_far,
        (nows, laters, (last,) + (-1,) * (FAR - 1)),
    )
    for unit in range(FAR):
        for across in range(0, CS, WIDE):
            for start in range(0, CS, STEP):
                retire(unit, lasts[unit], start, across)

    tiles = CS // 128
    for k in range(clusters):
        both = acc[k, 0:8, :] + acc[k, 8:16, :]
        block = main[me, k]
        turned = pltpu.roll(block, 5, 0)
        real = jnp.sum(jnp.where(rows < 3, both * turned, 0.0), axis=0, keepdims=True)
        imag = jnp.sum(
            jnp.where((rows > 2) & (rows < 6), both * block, 0.0), axis=0, keepdims=True
        )
        for row, value in enumerate((real, imag)):
            for part, piece in enumerate(split_three(value)):
                for tile in range(tiles):
                    base = (part * 2 + row) * clusters * tiles + k * tiles + tile
                    stack[base : base + 1, :] = piece[:, 128 * tile : 128 * tile + 128]
    slots = slot[...]
    lanes = lax.rem(slots, 128)
    chosen = jnp.where(
        lax.broadcasted_iota(jnp.int32, (128, local), 0) == lanes, 1.0, 0.0
    ).astype(BF16)
    spread = dot_nn(stack[...].astype(BF16), chosen)
    height = clusters * tiles
    mine = lax.broadcasted_iota(jnp.int32, (height, local), 0) == slots // 128
    induced = []
    for row in range(2):
        whole = 0.0
        for part in range(3):
            base = (part * 2 + row) * height
            whole = whole + spread[base : base + height]
        induced.append(jnp.sum(jnp.where(mine, whole, 0.0), axis=0, keepdims=True))
    scaled = resist[...] * cur[...]
    out[0:1, :] = scaled[0:1] - induced[1]
    out[1:2, :] = scaled[1:2] + induced[0]


def pair_terms(main, extra, resist, currents, slot_of):
    clusters = main.shape[1]
    return pl.pallas_call(
        pair_kernel,
        out_shape=jax.ShapeDtypeStruct(currents.shape, F32),
        in_specs=[VMEM] * 5,
        out_specs=VMEM,
        scratch_shapes=[
            pltpu.VMEM((clusters, 16, CS), F32),
            pltpu.VMEM((clusters, 3, 48, CS), BF16),
            pltpu.VMEM((FAR, 2, CS, 48), BF16),
            pltpu.VMEM((FAR, 16, CS), BF16),
            pltpu.VMEM((FAR, 16, CS), BF16),
            pltpu.VMEM((FAR, CS // STEP, 2 * STEP, CS), BF16),
            pltpu.VMEM((6 * clusters * CS // 128, 128), F32),
        ],
    )(main, extra, resist[None, :], currents, slot_of[None, :])


def gather_kernel(
    pos, seg, rad, cur, slot, pair, flag, main_all, extra_all, stack, send_sem, recv_sem
):
    row_count, col_count = lax.axis_size("row"), lax.axis_size("col")
    row, col = lax.axis_index("row"), lax.axis_index("col")
    me = row * col_count + col
    chips = row_count // 2
    other = row + 1 - 2 * lax.rem(row, 2)
    gathered = (main_all, extra_all)

    def row_at(base, step):
        return lax.rem(base + 2 * step, row_count)

    def col_at(step):
        return lax.rem(col + step, col_count)

    barrier = pltpu.get_barrier_semaphore()
    peers = [(row, col_at(k)) for k in range(1, col_count)]
    peers += [(row_at(row, k), col) for k in range(1, chips)] + [(other, col)]
    for to_row, to_col in peers:
        pl.semaphore_signal(
            barrier, inc=1, device_id={"row": to_row, "col": to_col}, device_id_type=MESH
        )
    order_into(
        pos, seg, rad, cur, slot, pair, flag, main_all.at[me], extra_all.at[me], stack
    )
    pl.semaphore_wait(barrier, len(peers))

    def copies(origin, lane, to_row, to_col):
        return [
            pltpu.make_async_remote_copy(
                src_ref=target.at[origin],
                dst_ref=target.at[origin],
                send_sem=send_sem.at[part, lane],
                recv_sem=recv_sem.at[part, origin],
                device_id={"row": to_row, "col": to_col},
                device_id_type=MESH,
            )
            for part, target in enumerate(gathered)
        ]

    sent = []

    def push(origin, to_row, to_col):
        started = copies(origin, len(sent), to_row, to_col)
        for copy in started:
            copy.start()
        sent.append(started)

    def arrive(origin):
        for copy in copies(origin, 0, other, col):
            copy.wait_recv()

    def fan_out(origin):
        for k in range(1, chips):
            push(origin, row_at(row, k), col)
        push(origin, other, col)

    for k in range(1, col_count):
        push(me, row, col_at(k))
    fan_out(me)
    for k in range(1, col_count):
        origin = row * col_count + col_at(col_count - k)
        arrive(origin)
        fan_out(origin)
    for block in range(col_count):
        for k in range(1, chips):
            origin = row_at(row, chips - k) * col_count + col_at(col_count - block)
            arrive(origin)
            push(origin, other, col)
    for block in range(col_count):
        for k in range(chips):
            arrive(row_at(other, chips - k) * col_count + col_at(col_count - block))
    for started in sent:
        for copy in started:
            copy.wait_send()


def gather_all(positions, segments, radius, currents, slot_of, pair_list, near_flag):
    row_count, col_count = lax.axis_size("row"), lax.axis_size("col")
    devices = row_count * col_count
    local = positions.shape[1]
    clusters = local // CS
    lanes = col_count - 1 + col_count * (row_count - 1)
    return pl.pallas_call(
        gather_kernel,
        out_shape=(
            jax.ShapeDtypeStruct((devices, clusters, 8, CS), F32),
            jax.ShapeDtypeStruct((devices, clusters + 2, CS), F32),
        ),
        in_specs=[VMEM] * 7,
        out_specs=(VMEM, VMEM),
        scratch_shapes=[
            pltpu.VMEM((48, local), F32),
            pltpu.SemaphoreType.DMA((2, lanes)),
            pltpu.SemaphoreType.DMA((2, devices)),
        ],
        compiler_params=pltpu.CompilerParams(collective_id=0, has_side_effects=True),
    )(
        positions,
        segments,
        radius[None, :],
        currents,
        slot_of[None, :],
        pair_list.T,
        near_flag[None, :],
    )


def on_device(positions, segments, radius, currents, resist, slot_of, pair_list, near_flag):
    main_all, extra_all = gather_all(
        positions, segments, radius, currents, slot_of, pair_list, near_flag
    )
    return pair_terms(main_all, extra_all, resist, currents, slot_of)


def solution(mesh):
    return jax.shard_map(
        on_device,
        mesh=mesh,
        in_specs=(
            P(None, ("row", "col")),
            P(None, ("row", "col")),
            P(("row", "col")),
            P(None, ("row", "col")),
            P(("row", "col")),
            P(("row", "col")),
            P(("row", "col"), None),
            P(("row", "col")),
        ),
        out_specs=P(None, ("row", "col")),
        check_vma=False,
    )
```

```python
import functools
import math

import jax
import jax.numpy as jnp
from jax import lax
from jax.experimental import pallas as pl
from jax.experimental.pallas import tpu as pltpu
from jax.sharding import PartitionSpec as P

CS = 512
F32 = jnp.float32
BF16 = jnp.bfloat16
MESH = pl.DeviceIdType.MESH
gauss_step = 0.5 / math.sqrt(3.0)
kernel_gain = 0.25
VMEM = pl.BlockSpec(memory_space=pltpu.VMEM)
WIDE = 256
STEP = 128
FAR = 2


def split_three(value):
    high = value.astype(BF16).astype(F32)
    rest = value - high
    middle = rest.astype(BF16).astype(F32)
    return high, middle, rest - middle


def dot_nn(left, right):
    return lax.dot_general(left, right, (((1,), (0,)), ((), ())), preferred_element_type=F32)


def dot_nt(left, right):
    return lax.dot_general(left, right, (((1,), (1,)), ((), ())), preferred_element_type=F32)


def one_hot_rows(slots, start, count):
    rows = lax.broadcasted_iota(jnp.int32, (count, slots.shape[1]), 0) + start
    return jnp.where(rows == slots, 1.0, 0.0).astype(BF16)


def order_into(pos, seg, rad, cur, slot, pair, flag, main, extra, stack):
    clusters = main.shape[0]
    slots = slot[...]
    stack[...] = jnp.zeros_like(stack)
    for source, row in ((pos, 0), (seg, 3), (rad, 6), (cur, 7)):
        count = source.shape[0]
        for part, piece in enumerate(split_three(source[...])):
            stack[part * 16 + row : part * 16 + row + count, :] = piece
    parts = stack[...].astype(BF16)
    for cluster in range(clusters):
        sums = dot_nt(parts, one_hot_rows(slots, cluster * CS, CS))
        ordered = sums[0:16] + sums[16:32] + sums[32:48]
        main[cluster] = ordered[0:8]
        extra[cluster : cluster + 1, :] = ordered[8:9]
    listed = pair.shape[1]
    extra[clusters : clusters + 2, :] = jnp.zeros((2, CS), F32)
    extra[clusters : clusters + 1, 0:listed] = pair[0:1, :].astype(F32)
    extra[clusters : clusters + 1, 128 : 128 + listed] = pair[1:2, :].astype(F32)
    extra[clusters : clusters + 1, 256 : 256 + listed] = flag[...].astype(F32)


def tile_rows(count):
    return lax.broadcasted_iota(jnp.int32, (8, count), 0)


def pair_kernel(
    main, extra, resist, cur, slot, out,
    acc, target, source, weight, retired, inverse, stack,
):
    devices, clusters = main.shape[0], main.shape[1]
    local = cur.shape[1]
    me = lax.axis_index("row") * lax.axis_size("col") + lax.axis_index("col")
    acc[...] = jnp.zeros_like(acc)
    rows = tile_rows(CS)

    lists = extra[:, clusters, :]
    first_ids, second_ids, flags = lists[:, 0:128], lists[:, 128:256], lists[:, 256:384]
    near_masks, far_masks, codes = [], [], []
    for k in range(clusters):
        own = (me * clusters + k).astype(F32)
        is_first = first_ids == own
        match = jnp.where(is_first | (second_ids == own), flags, 0.0)
        near_masks.append(jnp.where(match > 1.5, 1.0, 0.0))
        far_masks.append(jnp.where((match > 0.5) & (match < 1.5), 1.0, 0.0))
        codes.append(jnp.where(is_first, second_ids, first_ids) + 4096.0 * k)
    masks = jnp.concatenate(near_masks + far_masks, 0)
    code = jnp.concatenate(codes + codes, 0)
    marks = masks.astype(BF16)
    entries = masks.shape[0]
    before_lane = jnp.where(
        lax.broadcasted_iota(jnp.int32, (128, 128), 0) < lax.broadcasted_iota(jnp.int32, (128, 128), 1),
        1.0,
        0.0,
    ).astype(BF16)
    before_row = jnp.where(
        lax.broadcasted_iota(jnp.int32, (entries, entries), 1)
        < lax.broadcasted_iota(jnp.int32, (entries, entries), 0),
        1.0,
        0.0,
    ).astype(BF16)
    in_row = dot_nn(marks, jnp.ones((128, 128), BF16)).astype(BF16)
    rank = jnp.where(
        masks > 0.5, dot_nn(marks, before_lane) + dot_nn(before_row, in_row), -1.0
    ).astype(jnp.int32)
    near_count = jnp.sum(masks[0 : clusters * devices]).astype(jnp.int32)
    count = jnp.sum(masks).astype(jnp.int32)

    def pick(turn):
        return jnp.sum(jnp.where(rank == turn, code, 0.0)).astype(jnp.int32)

    def moved(block, turned, sign):
        points = block - 0.5
        if sign:
            points = points + (sign * gauss_step) * turned
        squares = jnp.where(rows < 3, points * points, jnp.where(rows == 3, turned * turned, 0.0))
        return points, jnp.sum(squares, axis=0, keepdims=True)

    def stacked(value, order):
        parts = split_three(value)
        return [
            jnp.concatenate([parts[order[n]], parts[order[n + 1]]], 0) for n in range(0, 6, 2)
        ]

    def source_side(points, norm):
        value = jnp.where(
            rows < 3, -2.0 * points, jnp.where(rows == 3, 1.0, jnp.where(rows == 4, norm, 0.0))
        )
        return jnp.concatenate(stacked(value, (0, 1, 0, 1, 2, 0)), 0)

    def target_side(points, norm):
        value = jnp.where(rows < 3, points, jnp.where(rows == 3, norm, jnp.where(rows == 4, 1.0, 0.0)))
        return jnp.concatenate(stacked(value, (0, 0, 1, 1, 0, 2)), 0)

    def prepare(unit, now, scale, signs):
        cluster = now % 4096
        device, place = cluster // clusters, cluster % clusters
        block = main[device, place]
        imag = extra[device, pl.ds(place, 1), :]
        turned = pltpu.roll(block, 5, 0)
        for index, sign in enumerate(signs):
            side = source_side(*moved(block, turned, sign))
            source[unit, index] = side.T.astype(BF16)
        value = jnp.where(rows < 3, turned * block[7:8], jnp.where(rows < 6, block * imag, 0.0))
        value = value * scale
        high = value.astype(BF16).astype(F32)
        weight[unit] = jnp.concatenate([high, value - high], 0).astype(BF16)

    def retire(unit, k, start, across):
        weights = retired[unit, :, start : start + STEP]
        term = dot_nn(
            jnp.concatenate([weights, weights], 1),
            inverse[unit, start // STEP, :, across : across + WIDE],
        )
        place = jnp.maximum(k, 0)
        acc[place, :, across : across + WIDE] += jnp.where(k >= 0, term, 0.0)

    def compute(unit, k, last, targets, sources):
        sides = [target[k, index] for index in targets]
        for across in range(0, CS, WIDE):
            for start in range(0, CS, STEP):
                retire(unit, last, start, across)
                total = 0.0
                for index in range(sources):
                    one = source[unit, index, start : start + STEP, :]
                    for side in sides:
                        total = total + lax.rsqrt(dot_nn(one, side[:, across : across + WIDE]))
                high = total.astype(BF16)
                low = (total - high.astype(F32)).astype(BF16)
                inverse[unit, start // STEP, 0:STEP, across : across + WIDE] = high
                inverse[unit, start // STEP, STEP:, across : across + WIDE] = low
        retired[unit] = weight[unit]

    for k in range(clusters):
        block = main[me, k]
        turned = pltpu.roll(block, 5, 0)
        for index, sign in enumerate((0, -1, 1)):
            target[k, index] = target_side(*moved(block, turned, sign)).astype(BF16)

    near_gain, far_gain = kernel_gain * 0.25, kernel_gain

    def visit_near(turn, state):
        now, later, last = state
        k = now // 4096
        compute(0, k, last, (1, 2), 2)
        prepare(0, later, near_gain, (-1, 1))
        return later, pick(turn + 2), k

    def far_scale(turn):
        return jnp.where(turn < count, far_gain, 0.0)

    def visit_far(step, state):
        turn = near_count + FAR * step
        nows, laters, lasts = state
        ks = tuple(nows[unit] // 4096 for unit in range(FAR))
        for unit in range(FAR):
            compute(unit, ks[unit], lasts[unit], (0,), 1)
        for unit in range(FAR):
            prepare(unit, laters[unit], far_scale(turn + FAR + unit), (0,))
        return laters, tuple(pick(turn + 2 * FAR + unit) for unit in range(FAR)), ks

    begin = pick(0)
    prepare(0, begin, near_gain, (-1, 1))
    _, _, last = lax.fori_loop(0, near_count, visit_near, (begin, pick(1), -1))
    nows = tuple(pick(near_count + unit) for unit in range(FAR))
    laters = tuple(pick(near_count + FAR + unit) for unit in range(FAR))
    for unit in range(FAR):
        prepare(unit, nows[unit], far_scale(near_count + unit), (0,))
    _, _, lasts = lax.fori_loop(
        0,
        (count - near_count + FAR - 1) // FAR,
        visit_far,
        (nows, laters, (last,) + (-1,) * (FAR - 1)),
    )
    for unit in range(FAR):
        for across in range(0, CS, WIDE):
            for start in range(0, CS, STEP):
                retire(unit, lasts[unit], start, across)

    tiles = CS // 128
    for k in range(clusters):
        both = acc[k, 0:8, :] + acc[k, 8:16, :]
        block = main[me, k]
        turned = pltpu.roll(block, 5, 0)
        real = jnp.sum(jnp.where(rows < 3, both * turned, 0.0), axis=0, keepdims=True)
        imag = jnp.sum(
            jnp.where((rows > 2) & (rows < 6), both * block, 0.0), axis=0, keepdims=True
        )
        for row, value in enumerate((real, imag)):
            for part, piece in enumerate(split_three(value)):
                for tile in range(tiles):
                    base = (part * 2 + row) * clusters * tiles + k * tiles + tile
                    stack[base : base + 1, :] = piece[:, 128 * tile : 128 * tile + 128]
    slots = slot[...]
    lanes = lax.rem(slots, 128)
    chosen = jnp.where(
        lax.broadcasted_iota(jnp.int32, (128, local), 0) == lanes, 1.0, 0.0
    ).astype(BF16)
    spread = dot_nn(stack[...].astype(BF16), chosen)
    height = clusters * tiles
    mine = lax.broadcasted_iota(jnp.int32, (height, local), 0) == slots // 128
    induced = []
    for row in range(2):
        whole = 0.0
        for part in range(3):
            base = (part * 2 + row) * height
            whole = whole + spread[base : base + height]
        induced.append(jnp.sum(jnp.where(mine, whole, 0.0), axis=0, keepdims=True))
    scaled = resist[...] * cur[...]
    out[0:1, :] = scaled[0:1] - induced[1]
    out[1:2, :] = scaled[1:2] + induced[0]


def pair_terms(main, extra, resist, currents, slot_of):
    clusters = main.shape[1]
    return pl.pallas_call(
        pair_kernel,
        out_shape=jax.ShapeDtypeStruct(currents.shape, F32),
        in_specs=[VMEM] * 5,
        out_specs=VMEM,
        scratch_shapes=[
            pltpu.VMEM((clusters, 16, CS), F32),
            pltpu.VMEM((clusters, 3, 48, CS), BF16),
            pltpu.VMEM((FAR, 2, CS, 48), BF16),
            pltpu.VMEM((FAR, 16, CS), BF16),
            pltpu.VMEM((FAR, 16, CS), BF16),
            pltpu.VMEM((FAR, CS // STEP, 2 * STEP, CS), BF16),
            pltpu.VMEM((6 * clusters * CS // 128, 128), F32),
        ],
        compiler_params=pltpu.CompilerParams(vmem_limit_bytes=24 << 20),
    )(main, extra, resist[None, :], currents, slot_of[None, :])


def gather_kernel(
    pos, seg, rad, cur, slot, pair, flag, main_all, extra_all, stack, send_sem, recv_sem
):
    row_count, col_count = lax.axis_size("row"), lax.axis_size("col")
    row, col = lax.axis_index("row"), lax.axis_index("col")
    me = row * col_count + col
    chips = row_count // 2
    other = row + 1 - 2 * lax.rem(row, 2)
    gathered = (main_all, extra_all)

    def row_at(base, step):
        return lax.rem(base + 2 * step, row_count)

    def col_at(step):
        return lax.rem(col + step, col_count)

    barrier = pltpu.get_barrier_semaphore()
    peers = [(row, col_at(k)) for k in range(1, col_count)]
    peers += [(row_at(row, k), col) for k in range(1, chips)] + [(other, col)]
    for to_row, to_col in peers:
        pl.semaphore_signal(
            barrier, inc=1, device_id={"row": to_row, "col": to_col}, device_id_type=MESH
        )
    order_into(
        pos, seg, rad, cur, slot, pair, flag, main_all.at[me], extra_all.at[me], stack
    )
    pl.semaphore_wait(barrier, len(peers))

    def copies(origin, lane, to_row, to_col):
        return [
            pltpu.make_async_remote_copy(
                src_ref=target.at[origin],
                dst_ref=target.at[origin],
                send_sem=send_sem.at[part, lane],
                recv_sem=recv_sem.at[part, origin],
                device_id={"row": to_row, "col": to_col},
                device_id_type=MESH,
            )
            for part, target in enumerate(gathered)
        ]

    sent = []

    def push(origin, to_row, to_col):
        started = copies(origin, len(sent), to_row, to_col)
        for copy in started:
            copy.start()
        sent.append(started)

    def arrive(origin):
        for copy in copies(origin, 0, other, col):
            copy.wait_recv()

    def fan_out(origin):
        for k in range(1, chips):
            push(origin, row_at(row, k), col)
        push(origin, other, col)

    for k in range(1, col_count):
        push(me, row, col_at(k))
    fan_out(me)
    for k in range(1, col_count):
        origin = row * col_count + col_at(col_count - k)
        arrive(origin)
        fan_out(origin)
    for block in range(col_count):
        for k in range(1, chips):
            origin = row_at(row, chips - k) * col_count + col_at(col_count - block)
            arrive(origin)
            push(origin, other, col)
    for block in range(col_count):
        for k in range(chips):
            arrive(row_at(other, chips - k) * col_count + col_at(col_count - block))
    for started in sent:
        for copy in started:
            copy.wait_send()


def gather_all(positions, segments, radius, currents, slot_of, pair_list, near_flag):
    row_count, col_count = lax.axis_size("row"), lax.axis_size("col")
    devices = row_count * col_count
    local = positions.shape[1]
    clusters = local // CS
    lanes = col_count - 1 + col_count * (row_count - 1)
    return pl.pallas_call(
        gather_kernel,
        out_shape=(
            jax.ShapeDtypeStruct((devices, clusters, 8, CS), F32),
            jax.ShapeDtypeStruct((devices, clusters + 2, CS), F32),
        ),
        in_specs=[VMEM] * 7,
        out_specs=(VMEM, VMEM),
        scratch_shapes=[
            pltpu.VMEM((48, local), F32),
            pltpu.SemaphoreType.DMA((2, lanes)),
            pltpu.SemaphoreType.DMA((2, devices)),
        ],
        compiler_params=pltpu.CompilerParams(
            collective_id=0, has_side_effects=True, vmem_limit_bytes=24 << 20
        ),
    )(
        positions,
        segments,
        radius[None, :],
        currents,
        slot_of[None, :],
        pair_list.T,
        near_flag[None, :],
    )


def on_device(positions, segments, radius, currents, resist, slot_of, pair_list, near_flag):
    main_all, extra_all = gather_all(
        positions, segments, radius, currents, slot_of, pair_list, near_flag
    )
    return pair_terms(main_all, extra_all, resist, currents, slot_of)


def solution(mesh):
    return jax.shard_map(
        on_device,
        mesh=mesh,
        in_specs=(
            P(None, ("row", "col")),
            P(None, ("row", "col")),
            P(("row", "col")),
            P(None, ("row", "col")),
            P(("row", "col")),
            P(("row", "col")),
            P(("row", "col"), None),
            P(("row", "col")),
        ),
        out_specs=P(None, ("row", "col")),
        check_vma=False,
    )
```

```python
import functools
import math

import jax
import jax.numpy as jnp
from jax import lax
from jax.experimental import pallas as pl
from jax.experimental.pallas import tpu as pltpu
from jax.sharding import PartitionSpec as P

CS = 512
F32 = jnp.float32
BF16 = jnp.bfloat16
MESH = pl.DeviceIdType.MESH
gauss_step = 0.5 / math.sqrt(3.0)
kernel_gain = 0.25
VMEM = pl.BlockSpec(memory_space=pltpu.VMEM)
HBM = pl.BlockSpec(memory_space=pltpu.HBM)
TILES = CS // 128
LIST = 9 * TILES
WIDE = 256
STEP = 128
FAR = 2


def split_three(value):
    high = value.astype(BF16).astype(F32)
    rest = value - high
    middle = rest.astype(BF16).astype(F32)
    return high, middle, rest - middle


def dot_nn(left, right):
    return lax.dot_general(left, right, (((1,), (0,)), ((), ())), preferred_element_type=F32)


def dot_nt(left, right):
    return lax.dot_general(left, right, (((1,), (1,)), ((), ())), preferred_element_type=F32)


def one_hot_rows(slots, start, count):
    rows = lax.broadcasted_iota(jnp.int32, (count, slots.shape[1]), 0) + start
    return jnp.where(rows == slots, 1.0, 0.0).astype(BF16)


def order_into(pos, seg, rad, cur, slot, pair, flag, packed, stack):
    clusters = packed.shape[0]
    slots = slot[...]
    stack[...] = jnp.zeros_like(stack)
    for source, row in ((pos, 0), (seg, 3), (rad, 6), (cur, 7)):
        count = source.shape[0]
        for part, piece in enumerate(split_three(source[...])):
            stack[part * 16 + row : part * 16 + row + count, :] = piece
    parts = stack[...].astype(BF16)
    for cluster in range(clusters):
        sums = dot_nt(parts, one_hot_rows(slots, cluster * CS, CS))
        ordered = sums[0:16] + sums[16:32] + sums[32:48]
        packed[cluster, 8 * TILES :, :] = jnp.zeros((8, 128), F32)
        for tile in range(TILES):
            lanes = slice(128 * tile, 128 * tile + 128)
            packed[cluster, 8 * tile : 8 * tile + 8, :] = ordered[0:8, lanes]
            packed[cluster, 8 * TILES + tile : 8 * TILES + tile + 1, :] = ordered[8:9, lanes]
    code = (pair[0:1, :] * 1024 + pair[1:2, :]) * 4 + flag[...]
    packed[0, LIST : LIST + 1, 0 : pair.shape[1]] = code.astype(F32)


def rows_of(packed, device, cluster):
    block = jnp.concatenate(
        [packed[device, cluster, 8 * tile : 8 * tile + 8, :] for tile in range(TILES)], 1
    )
    first = 8 * TILES
    imag = jnp.concatenate(
        [packed[device, cluster, first + tile : first + tile + 1, :] for tile in range(TILES)], 1
    )
    return block, imag


def tile_rows(count):
    return lax.broadcasted_iota(jnp.int32, (8, count), 0)


def pair_kernel(
    packed, resist_in, cur_in, slot_in, out,
    acc, target, source, weight, retired, inverse, stack, resist, cur, slot, sems,
):
    devices, clusters = packed.shape[0], packed.shape[1]
    local = cur.shape[1]
    loads = [
        pltpu.make_async_copy(outer, inner, sems.at[index])
        for index, (outer, inner) in enumerate(
            ((resist_in, resist), (cur_in, cur), (slot_in, slot))
        )
    ]
    for load in loads:
        load.start()
    me = lax.axis_index("row") * lax.axis_size("col") + lax.axis_index("col")
    acc[...] = jnp.zeros_like(acc)
    rows = tile_rows(CS)

    lists = packed[:, 0, LIST, :].astype(jnp.int32)
    first_ids, second_ids = lists // 4096, lists // 4 % 1024
    flags = (lists % 4).astype(F32)
    near_masks, far_masks, codes = [], [], []
    for k in range(clusters):
        own = me * clusters + k
        is_first = first_ids == own
        match = jnp.where(is_first | (second_ids == own), flags, 0.0)
        near_masks.append(jnp.where(match > 1.5, 1.0, 0.0))
        far_masks.append(jnp.where((match > 0.5) & (match < 1.5), 1.0, 0.0))
        codes.append(jnp.where(is_first, second_ids, first_ids).astype(F32) + 4096.0 * k)
    masks = jnp.concatenate(near_masks + far_masks, 0)
    code = jnp.concatenate(codes + codes, 0)
    marks = masks.astype(BF16)
    entries = masks.shape[0]
    before_lane = jnp.where(
        lax.broadcasted_iota(jnp.int32, (128, 128), 0) < lax.broadcasted_iota(jnp.int32, (128, 128), 1),
        1.0,
        0.0,
    ).astype(BF16)
    before_row = jnp.where(
        lax.broadcasted_iota(jnp.int32, (entries, entries), 1)
        < lax.broadcasted_iota(jnp.int32, (entries, entries), 0),
        1.0,
        0.0,
    ).astype(BF16)
    in_row = dot_nn(marks, jnp.ones((128, 128), BF16)).astype(BF16)
    rank = jnp.where(
        masks > 0.5, dot_nn(marks, before_lane) + dot_nn(before_row, in_row), -1.0
    ).astype(jnp.int32)
    near_count = jnp.sum(masks[0 : clusters * devices]).astype(jnp.int32)
    count = jnp.sum(masks).astype(jnp.int32)

    def pick(turn):
        return jnp.sum(jnp.where(rank == turn, code, 0.0)).astype(jnp.int32)

    def moved(block, turned, sign):
        points = block - 0.5
        if sign:
            points = points + (sign * gauss_step) * turned
        squares = jnp.where(rows < 3, points * points, jnp.where(rows == 3, turned * turned, 0.0))
        return points, jnp.sum(squares, axis=0, keepdims=True)

    def stacked(value, order):
        parts = split_three(value)
        return [
            jnp.concatenate([parts[order[n]], parts[order[n + 1]]], 0) for n in range(0, 6, 2)
        ]

    def source_side(points, norm):
        value = jnp.where(
            rows < 3, -2.0 * points, jnp.where(rows == 3, 1.0, jnp.where(rows == 4, norm, 0.0))
        )
        return jnp.concatenate(stacked(value, (0, 1, 0, 1, 2, 0)), 0)

    def target_side(points, norm):
        value = jnp.where(rows < 3, points, jnp.where(rows == 3, norm, jnp.where(rows == 4, 1.0, 0.0)))
        return jnp.concatenate(stacked(value, (0, 0, 1, 1, 0, 2)), 0)

    def prepare(unit, now, scale, signs):
        cluster = now % 4096
        device, place = cluster // clusters, cluster % clusters
        block, imag = rows_of(packed, device, place)
        turned = pltpu.roll(block, 5, 0)
        for index, sign in enumerate(signs):
            side = source_side(*moved(block, turned, sign))
            source[unit, index] = side.T.astype(BF16)
        value = jnp.where(rows < 3, turned * block[7:8], jnp.where(rows < 6, block * imag, 0.0))
        value = value * scale
        high = value.astype(BF16).astype(F32)
        weight[unit] = jnp.concatenate([high, value - high], 0).astype(BF16)

    def retire(unit, k, start, across):
        weights = retired[unit, :, start : start + STEP]
        term = dot_nn(
            jnp.concatenate([weights, weights], 1),
            inverse[unit, start // STEP, :, across : across + WIDE],
        )
        place = jnp.maximum(k, 0)
        acc[place, :, across : across + WIDE] += jnp.where(k >= 0, term, 0.0)

    def compute(unit, k, last, targets, sources):
        sides = [target[k, index] for index in targets]
        for across in range(0, CS, WIDE):
            for start in range(0, CS, STEP):
                retire(unit, last, start, across)
                total = 0.0
                for index in range(sources):
                    one = source[unit, index, start : start + STEP, :]
                    for side in sides:
                        total = total + lax.rsqrt(dot_nn(one, side[:, across : across + WIDE]))
                high = total.astype(BF16)
                low = (total - high.astype(F32)).astype(BF16)
                inverse[unit, start // STEP, 0:STEP, across : across + WIDE] = high
                inverse[unit, start // STEP, STEP:, across : across + WIDE] = low
        retired[unit] = weight[unit]

    for k in range(clusters):
        block, _ = rows_of(packed, me, k)
        turned = pltpu.roll(block, 5, 0)
        for index, sign in enumerate((0, -1, 1)):
            target[k, index] = target_side(*moved(block, turned, sign)).astype(BF16)

    near_gain, far_gain = kernel_gain * 0.25, kernel_gain

    def visit_near(turn, state):
        now, later, last = state
        k = now // 4096
        compute(0, k, last, (1, 2), 2)
        prepare(0, later, near_gain, (-1, 1))
        return later, pick(turn + 2), k

    def far_scale(turn):
        return jnp.where(turn < count, far_gain, 0.0)

    def visit_far(step, state):
        turn = near_count + FAR * step
        nows, laters, lasts = state
        ks = tuple(nows[unit] // 4096 for unit in range(FAR))
        for unit in range(FAR):
            compute(unit, ks[unit], lasts[unit], (0,), 1)
        for unit in range(FAR):
            prepare(unit, laters[unit], far_scale(turn + FAR + unit), (0,))
        return laters, tuple(pick(turn + 2 * FAR + unit) for unit in range(FAR)), ks

    begin = pick(0)
    prepare(0, begin, near_gain, (-1, 1))
    _, _, last = lax.fori_loop(0, near_count, visit_near, (begin, pick(1), -1))
    nows = tuple(pick(near_count + unit) for unit in range(FAR))
    laters = tuple(pick(near_count + FAR + unit) for unit in range(FAR))
    for unit in range(FAR):
        prepare(unit, nows[unit], far_scale(near_count + unit), (0,))
    _, _, lasts = lax.fori_loop(
        0,
        (count - near_count + FAR - 1) // FAR,
        visit_far,
        (nows, laters, (last,) + (-1,) * (FAR - 1)),
    )
    for unit in range(FAR):
        for across in range(0, CS, WIDE):
            for start in range(0, CS, STEP):
                retire(unit, lasts[unit], start, across)

    tiles = CS // 128
    for k in range(clusters):
        both = acc[k, 0:8, :] + acc[k, 8:16, :]
        block, _ = rows_of(packed, me, k)
        turned = pltpu.roll(block, 5, 0)
        real = jnp.sum(jnp.where(rows < 3, both * turned, 0.0), axis=0, keepdims=True)
        imag = jnp.sum(
            jnp.where((rows > 2) & (rows < 6), both * block, 0.0), axis=0, keepdims=True
        )
        for row, value in enumerate((real, imag)):
            for part, piece in enumerate(split_three(value)):
                for tile in range(tiles):
                    base = (part * 2 + row) * clusters * tiles + k * tiles + tile
                    stack[base : base + 1, :] = piece[:, 128 * tile : 128 * tile + 128]
    for load in loads:
        load.wait()
    slots = slot[...]
    lanes = lax.rem(slots, 128)
    chosen = jnp.where(
        lax.broadcasted_iota(jnp.int32, (128, local), 0) == lanes, 1.0, 0.0
    ).astype(BF16)
    spread = dot_nn(stack[...].astype(BF16), chosen)
    height = clusters * tiles
    mine = lax.broadcasted_iota(jnp.int32, (height, local), 0) == slots // 128
    induced = []
    for row in range(2):
        whole = 0.0
        for part in range(3):
            base = (part * 2 + row) * height
            whole = whole + spread[base : base + height]
        induced.append(jnp.sum(jnp.where(mine, whole, 0.0), axis=0, keepdims=True))
    scaled = resist[...] * cur[...]
    out[0:1, :] = scaled[0:1] - induced[1]
    out[1:2, :] = scaled[1:2] + induced[0]


def pair_terms(packed, resist, currents, slot_of):
    clusters = packed.shape[1]
    local = currents.shape[1]
    return pl.pallas_call(
        pair_kernel,
        out_shape=jax.ShapeDtypeStruct(currents.shape, F32),
        in_specs=[VMEM] + [HBM] * 3,
        out_specs=VMEM,
        scratch_shapes=[
            pltpu.VMEM((clusters, 16, CS), F32),
            pltpu.VMEM((clusters, 3, 48, CS), BF16),
            pltpu.VMEM((FAR, 2, CS, 48), BF16),
            pltpu.VMEM((FAR, 16, CS), BF16),
            pltpu.VMEM((FAR, 16, CS), BF16),
            pltpu.VMEM((FAR, CS // STEP, 2 * STEP, CS), BF16),
            pltpu.VMEM((6 * clusters * CS // 128, 128), F32),
            pltpu.VMEM((1, local), F32),
            pltpu.VMEM((2, local), F32),
            pltpu.VMEM((1, local), jnp.int32),
            pltpu.SemaphoreType.DMA((3,)),
        ],
    )(packed, resist[None, :], currents, slot_of[None, :])


def gather_kernel(
    pos_in, seg_in, rad_in, cur_in, slot_in, pair_in, flag_in, packed,
    pos, seg, rad, cur, slot, pair, flag, stack, load_sem, send_sem, recv_sem,
):
    row_count, col_count = lax.axis_size("row"), lax.axis_size("col")
    row, col = lax.axis_index("row"), lax.axis_index("col")
    me = row * col_count + col
    clusters = packed.shape[1]
    dims = (row_count // 2).bit_length() - 1
    other = row + 1 - 2 * lax.rem(row, 2)
    loads = [
        pltpu.make_async_copy(outer, inner, load_sem.at[index])
        for index, (outer, inner) in enumerate(
            zip(
                (pos_in, seg_in, rad_in, cur_in, slot_in, pair_in, flag_in),
                (pos, seg, rad, cur, slot, pair, flag),
            )
        )
    ]
    for load in loads:
        load.start()

    def across(base, dim):
        size = 2 << dim
        return base + size * (1 - 2 * lax.rem(base // size, 2))

    def moved_by(base, bits):
        for dim in range(dims):
            if bits >> dim & 1:
                base = across(base, dim)
        return base

    barrier = pltpu.get_barrier_semaphore()
    peers = [(row, lax.rem(col + k, col_count)) for k in range(1, col_count)]
    peers += [(across(row, dim), col) for dim in range(dims)] + [(other, col)]
    for to_row, to_col in peers:
        pl.semaphore_signal(
            barrier, inc=1, device_id={"row": to_row, "col": to_col}, device_id_type=MESH
        )
    for load in loads:
        load.wait()
    order_into(pos, seg, rad, cur, slot, pair, flag, packed.at[me], stack)
    pl.semaphore_wait(barrier, len(peers))

    def copy_of(origin, piece, lane, to_row, to_col):
        ref = packed.at[origin] if piece is None else packed.at[origin, piece]
        return pltpu.make_async_remote_copy(
            src_ref=ref,
            dst_ref=ref,
            send_sem=send_sem.at[lane],
            recv_sem=recv_sem.at[0 if piece is None else piece, origin],
            device_id={"row": to_row, "col": to_col},
            device_id_type=MESH,
        )

    sent = []

    def push(origin, piece, to_row, to_col, valid):
        copy_of(origin, piece, len(sent), to_row, to_col).start()
        sent.append((piece, valid))

    def arrive(origin, piece):
        copy_of(origin, piece, 0, other, col).wait_recv()

    def under(valid, act):
        if valid is None:
            act()
        else:
            pl.when(valid)(act)

    def order_of(piece):
        return [(piece + step) % dims for step in range(dims)]

    def later_dims(piece, bits):
        order = order_of(piece)
        last = max([n for n, dim in enumerate(order) if bits >> dim & 1], default=-1)
        return order[last + 1 :]

    pieces = range(clusters)

    def spread(place, valid):
        origin = row * col_count + place
        for step in range(dims):
            for piece in pieces:
                push(origin, piece, across(row, order_of(piece)[step]), col, valid)
        push(origin, None, other, col, valid)

    rest = sorted(range(1, 1 << dims), key=lambda bits: (bits.bit_count(), bits))

    def relay(place, valid):
        for bits in rest:
            origin = moved_by(row, bits) * col_count + place
            for piece in pieces:
                if later_dims(piece, bits):
                    arrive(origin, piece)
                    for dim in later_dims(piece, bits):
                        push(origin, piece, across(row, dim), col, valid)

    def share(place, valid):
        for bits in rest:
            origin = moved_by(row, bits) * col_count + place
            for piece in pieces:
                if not later_dims(piece, bits):
                    arrive(origin, piece)
            push(origin, None, other, col, valid)

    places = []
    for distance in range(1, col_count):
        for place in (col + distance, col - distance):
            places.append((place, (place >= 0) & (place < col_count)))
    for place, valid in places:
        under(valid, lambda: push(me, None, row, place, valid))
    spread(col, None)

    def enter(place, valid):
        arrive(row * col_count + place, None)
        spread(place, valid)

    stages = [(col, None)] + places
    for turn in range(0, len(places) + 4, 2):
        for place, valid in places[turn : turn + 2]:
            under(valid, lambda: enter(place, valid))
        for place, valid in stages[max(turn - 1, 0) : turn + 1]:
            under(valid, lambda: relay(place, valid))
        if turn >= 2:
            for place, valid in stages[max(turn - 3, 0) : turn - 1]:
                under(valid, lambda: share(place, valid))
    for bits in [0] + rest:
        for place, valid in stages:
            under(valid, lambda: arrive(moved_by(other, bits) * col_count + place, None))
    for lane, (piece, valid) in enumerate(sent):
        under(valid, lambda: copy_of(me, piece, lane, other, col).wait_send())


def gather_all(positions, segments, radius, currents, slot_of, pair_list, near_flag):
    row_count, col_count = lax.axis_size("row"), lax.axis_size("col")
    devices = row_count * col_count
    local = positions.shape[1]
    clusters = local // CS
    listed = near_flag.shape[0]
    lanes = 2 * col_count * (2 * row_count + 4 * clusters)
    return pl.pallas_call(
        gather_kernel,
        out_shape=jax.ShapeDtypeStruct((devices, clusters, LIST + 8 - TILES, 128), F32),
        in_specs=[HBM] * 7,
        out_specs=VMEM,
        scratch_shapes=[
            pltpu.VMEM((3, local), F32),
            pltpu.VMEM((3, local), F32),
            pltpu.VMEM((1, local), F32),
            pltpu.VMEM((2, local), F32),
            pltpu.VMEM((1, local), jnp.int32),
            pltpu.VMEM((2, listed), jnp.int32),
            pltpu.VMEM((1, listed), jnp.int32),
            pltpu.VMEM((48, local), F32),
            pltpu.SemaphoreType.DMA((7,)),
            pltpu.SemaphoreType.DMA((lanes,)),
            pltpu.SemaphoreType.DMA((clusters, devices)),
        ],
        compiler_params=pltpu.CompilerParams(
            collective_id=0, has_side_effects=True
        ),
    )(
        positions,
        segments,
        radius[None, :],
        currents,
        slot_of[None, :],
        pair_list.T,
        near_flag[None, :],
    )


def on_device(positions, segments, radius, currents, resist, slot_of, pair_list, near_flag):
    packed = gather_all(
        positions, segments, radius, currents, slot_of, pair_list, near_flag
    )
    return pair_terms(packed, resist, currents, slot_of)


def solution(mesh):
    return jax.shard_map(
        on_device,
        mesh=mesh,
        in_specs=(
            P(None, ("row", "col")),
            P(None, ("row", "col")),
            P(("row", "col")),
            P(None, ("row", "col")),
            P(("row", "col")),
            P(("row", "col")),
            P(("row", "col"), None),
            P(("row", "col")),
        ),
        out_specs=P(None, ("row", "col")),
        check_vma=False,
    )
```

```python
import functools
import math

import jax
import jax.numpy as jnp
from jax import lax
from jax.experimental import pallas as pl
from jax.experimental.pallas import tpu as pltpu
from jax.sharding import PartitionSpec as P

CS = 512
F32 = jnp.float32
BF16 = jnp.bfloat16
MESH = pl.DeviceIdType.MESH
gauss_step = 0.5 / math.sqrt(3.0)
kernel_gain = 0.25
VMEM = pl.BlockSpec(memory_space=pltpu.VMEM)
HBM = pl.BlockSpec(memory_space=pltpu.HBM)
WIDE = 256
STEP = 128
FAR = 2


def split_three(value):
    high = value.astype(BF16).astype(F32)
    rest = value - high
    middle = rest.astype(BF16).astype(F32)
    return high, middle, rest - middle


def dot_nn(left, right):
    return lax.dot_general(left, right, (((1,), (0,)), ((), ())), preferred_element_type=F32)


def dot_nt(left, right):
    return lax.dot_general(left, right, (((1,), (1,)), ((), ())), preferred_element_type=F32)


def one_hot_rows(slots, start, count):
    rows = lax.broadcasted_iota(jnp.int32, (count, slots.shape[1]), 0) + start
    return jnp.where(rows == slots, 1.0, 0.0).astype(BF16)


def order_into(pos, seg, rad, cur, slot, pair, flag, main, extra, stack):
    clusters = main.shape[0]
    slots = slot[...]
    stack[...] = jnp.zeros_like(stack)
    for source, row in ((pos, 0), (seg, 3), (rad, 6), (cur, 7)):
        count = source.shape[0]
        for part, piece in enumerate(split_three(source[...])):
            stack[part * 16 + row : part * 16 + row + count, :] = piece
    parts = stack[...].astype(BF16)
    for cluster in range(clusters):
        sums = dot_nt(parts, one_hot_rows(slots, cluster * CS, CS))
        ordered = sums[0:16] + sums[16:32] + sums[32:48]
        main[cluster] = ordered[0:8]
        extra[cluster : cluster + 1, :] = ordered[8:9]
    listed = pair.shape[1]
    extra[clusters : clusters + 2, :] = jnp.zeros((2, CS), F32)
    extra[clusters : clusters + 1, 0:listed] = pair[0:1, :].astype(F32)
    extra[clusters : clusters + 1, 128 : 128 + listed] = pair[1:2, :].astype(F32)
    extra[clusters : clusters + 1, 256 : 256 + listed] = flag[...].astype(F32)


def tile_rows(count):
    return lax.broadcasted_iota(jnp.int32, (8, count), 0)


def pair_kernel(
    main_in, extra_in, resist, cur, slot, out,
    acc, target, source, weight, retired, inverse, stack, main, extra, sems,
):
    devices, clusters = main.shape[0], main.shape[1]
    local = cur.shape[1]
    load_extra = pltpu.make_async_copy(extra_in, extra, sems.at[0])
    load_main = pltpu.make_async_copy(main_in, main, sems.at[1])
    load_extra.start()
    load_main.start()
    me = lax.axis_index("row") * lax.axis_size("col") + lax.axis_index("col")
    acc[...] = jnp.zeros_like(acc)
    rows = tile_rows(CS)

    load_extra.wait()
    lists = extra[:, clusters, :]
    first_ids, second_ids, flags = lists[:, 0:128], lists[:, 128:256], lists[:, 256:384]
    near_masks, far_masks, codes = [], [], []
    for k in range(clusters):
        own = (me * clusters + k).astype(F32)
        is_first = first_ids == own
        match = jnp.where(is_first | (second_ids == own), flags, 0.0)
        near_masks.append(jnp.where(match > 1.5, 1.0, 0.0))
        far_masks.append(jnp.where((match > 0.5) & (match < 1.5), 1.0, 0.0))
        codes.append(jnp.where(is_first, second_ids, first_ids) + 4096.0 * k)
    masks = jnp.concatenate(near_masks + far_masks, 0)
    code = jnp.concatenate(codes + codes, 0)
    marks = masks.astype(BF16)
    entries = masks.shape[0]
    before_lane = jnp.where(
        lax.broadcasted_iota(jnp.int32, (128, 128), 0) < lax.broadcasted_iota(jnp.int32, (128, 128), 1),
        1.0,
        0.0,
    ).astype(BF16)
    before_row = jnp.where(
        lax.broadcasted_iota(jnp.int32, (entries, entries), 1)
        < lax.broadcasted_iota(jnp.int32, (entries, entries), 0),
        1.0,
        0.0,
    ).astype(BF16)
    in_row = dot_nn(marks, jnp.ones((128, 128), BF16)).astype(BF16)
    rank = jnp.where(
        masks > 0.5, dot_nn(marks, before_lane) + dot_nn(before_row, in_row), -1.0
    ).astype(jnp.int32)
    near_count = jnp.sum(masks[0 : clusters * devices]).astype(jnp.int32)
    count = jnp.sum(masks).astype(jnp.int32)

    def pick(turn):
        return jnp.sum(jnp.where(rank == turn, code, 0.0)).astype(jnp.int32)

    def moved(block, turned, sign):
        points = block - 0.5
        if sign:
            points = points + (sign * gauss_step) * turned
        squares = jnp.where(rows < 3, points * points, jnp.where(rows == 3, turned * turned, 0.0))
        return points, jnp.sum(squares, axis=0, keepdims=True)

    def stacked(value, order):
        parts = split_three(value)
        return [
            jnp.concatenate([parts[order[n]], parts[order[n + 1]]], 0) for n in range(0, 6, 2)
        ]

    def source_side(points, norm):
        value = jnp.where(
            rows < 3, -2.0 * points, jnp.where(rows == 3, 1.0, jnp.where(rows == 4, norm, 0.0))
        )
        return jnp.concatenate(stacked(value, (0, 1, 0, 1, 2, 0)), 0)

    def target_side(points, norm):
        value = jnp.where(rows < 3, points, jnp.where(rows == 3, norm, jnp.where(rows == 4, 1.0, 0.0)))
        return jnp.concatenate(stacked(value, (0, 0, 1, 1, 0, 2)), 0)

    def prepare(unit, now, scale, signs):
        cluster = now % 4096
        device, place = cluster // clusters, cluster % clusters
        block = main[device, place]
        imag = extra[device, pl.ds(place, 1), :]
        turned = pltpu.roll(block, 5, 0)
        for index, sign in enumerate(signs):
            side = source_side(*moved(block, turned, sign))
            source[unit, index] = side.T.astype(BF16)
        value = jnp.where(rows < 3, turned * block[7:8], jnp.where(rows < 6, block * imag, 0.0))
        value = value * scale
        high = value.astype(BF16).astype(F32)
        weight[unit] = jnp.concatenate([high, value - high], 0).astype(BF16)

    def term_of(unit, start, across):
        weights = retired[unit, :, start : start + STEP]
        return dot_nn(
            jnp.concatenate([weights, weights], 1),
            inverse[unit, start // STEP, :, across : across + WIDE],
        )

    def retire(k, across, term):
        place = jnp.maximum(k, 0)
        acc[place, :, across : across + WIDE] += jnp.where(k >= 0, term, 0.0)

    def compute(unit, k, last, targets, sources):
        sides = [target[k, index] for index in targets]
        for across in range(0, CS, WIDE):
            term = 0.0
            for start in range(0, CS, STEP):
                term = term + term_of(unit, start, across)
                total = 0.0
                for index in range(sources):
                    one = source[unit, index, start : start + STEP, :]
                    for side in sides:
                        total = total + lax.rsqrt(dot_nn(one, side[:, across : across + WIDE]))
                high = total.astype(BF16)
                low = (total - high.astype(F32)).astype(BF16)
                inverse[unit, start // STEP, 0:STEP, across : across + WIDE] = high
                inverse[unit, start // STEP, STEP:, across : across + WIDE] = low
            retire(last, across, term)
        retired[unit] = weight[unit]

    load_main.wait()
    for k in range(clusters):
        block = main[me, k]
        turned = pltpu.roll(block, 5, 0)
        for index, sign in enumerate((0, -1, 1)):
            target[k, index] = target_side(*moved(block, turned, sign)).astype(BF16)

    near_gain, far_gain = kernel_gain * 0.25, kernel_gain

    def visit_near(turn, state):
        now, later, last = state
        k = now // 4096
        compute(0, k, last, (1, 2), 2)
        prepare(0, later, near_gain, (-1, 1))
        return later, pick(turn + 2), k

    def far_scale(turn):
        return jnp.where(turn < count, far_gain, 0.0)

    def visit_far(step, state):
        turn = near_count + FAR * step
        nows, laters, lasts = state
        ks = tuple(nows[unit] // 4096 for unit in range(FAR))
        for unit in range(FAR):
            compute(unit, ks[unit], lasts[unit], (0,), 1)
        for unit in range(FAR):
            prepare(unit, laters[unit], far_scale(turn + FAR + unit), (0,))
        return laters, tuple(pick(turn + 2 * FAR + unit) for unit in range(FAR)), ks

    begin = pick(0)
    prepare(0, begin, near_gain, (-1, 1))
    _, _, last = lax.fori_loop(0, near_count, visit_near, (begin, pick(1), -1))
    nows = tuple(pick(near_count + unit) for unit in range(FAR))
    laters = tuple(pick(near_count + FAR + unit) for unit in range(FAR))
    for unit in range(FAR):
        prepare(unit, nows[unit], far_scale(near_count + unit), (0,))
    _, _, lasts = lax.fori_loop(
        0,
        (count - near_count + FAR - 1) // FAR,
        visit_far,
        (nows, laters, (last,) + (-1,) * (FAR - 1)),
    )
    for unit in range(FAR):
        weights = retired[unit]
        doubled = []
        for start in range(0, CS, STEP):
            doubled += [weights[:, start : start + STEP]] * 2
        doubled = jnp.concatenate(doubled, 1)
        for across in range(0, CS, WIDE):
            tall = inverse[unit, :, :, across : across + WIDE].reshape(2 * CS, WIDE)
            retire(lasts[unit], across, dot_nn(doubled, tall))

    tiles = CS // 128
    for k in range(clusters):
        both = acc[k, 0:8, :] + acc[k, 8:16, :]
        block = main[me, k]
        turned = pltpu.roll(block, 5, 0)
        real = jnp.sum(jnp.where(rows < 3, both * turned, 0.0), axis=0, keepdims=True)
        imag = jnp.sum(
            jnp.where((rows > 2) & (rows < 6), both * block, 0.0), axis=0, keepdims=True
        )
        for row, value in enumerate((real, imag)):
            for part, piece in enumerate(split_three(value)):
                for tile in range(tiles):
                    base = (part * 2 + row) * clusters * tiles + k * tiles + tile
                    stack[base : base + 1, :] = piece[:, 128 * tile : 128 * tile + 128]
    slots = slot[...]
    lanes = lax.rem(slots, 128)
    chosen = jnp.where(
        lax.broadcasted_iota(jnp.int32, (128, local), 0) == lanes, 1.0, 0.0
    ).astype(BF16)
    spread = dot_nn(stack[...].astype(BF16), chosen)
    height = clusters * tiles
    mine = lax.broadcasted_iota(jnp.int32, (height, local), 0) == slots // 128
    induced = []
    for row in range(2):
        whole = 0.0
        for part in range(3):
            base = (part * 2 + row) * height
            whole = whole + spread[base : base + height]
        induced.append(jnp.sum(jnp.where(mine, whole, 0.0), axis=0, keepdims=True))
    scaled = resist[...] * cur[...]
    out[0:1, :] = scaled[0:1] - induced[1]
    out[1:2, :] = scaled[1:2] + induced[0]


def pair_terms(main, extra, resist, currents, slot_of):
    clusters = main.shape[1]
    return pl.pallas_call(
        pair_kernel,
        out_shape=jax.ShapeDtypeStruct(currents.shape, F32),
        in_specs=[HBM] * 2 + [VMEM] * 3,
        out_specs=VMEM,
        scratch_shapes=[
            pltpu.VMEM((clusters, 16, CS), F32),
            pltpu.VMEM((clusters, 3, 48, CS), BF16),
            pltpu.VMEM((FAR, 2, CS, 48), BF16),
            pltpu.VMEM((FAR, 16, CS), BF16),
            pltpu.VMEM((FAR, 16, CS), BF16),
            pltpu.VMEM((FAR, CS // STEP, 2 * STEP, CS), BF16),
            pltpu.VMEM((6 * clusters * CS // 128, 128), F32),
            pltpu.VMEM(main.shape, F32),
            pltpu.VMEM(extra.shape, F32),
            pltpu.SemaphoreType.DMA((2,)),
        ],
    )(main, extra, resist[None, :], currents, slot_of[None, :])


def gather_kernel(
    pos, seg, rad, cur, slot, pair, flag, main_out, extra_out,
    main_all, extra_all, stack, send_sem, recv_sem, store_sem,
):
    row_count, col_count = lax.axis_size("row"), lax.axis_size("col")
    row, col = lax.axis_index("row"), lax.axis_index("col")
    me = row * col_count + col
    chips = row_count // 2
    other = row + 1 - 2 * lax.rem(row, 2)
    gathered = (main_all, extra_all)

    def row_at(base, step):
        return lax.rem(base + 2 * step, row_count)

    def col_at(step):
        return lax.rem(col + step, col_count)

    def skipping(place, step):
        return step + 1 - (col_count + place - step - 1) // col_count

    def nearest(step):
        back = col_count - 1 - col
        upper = (2 * col) // col_count
        return (1 - upper) * skipping(col, step) + upper * (
            col_count - 1 - skipping(back, step)
        )

    barrier = pltpu.get_barrier_semaphore()
    peers = [(row, col_at(k)) for k in range(1, col_count)]
    peers += [(row_at(row, k), col) for k in range(1, chips)] + [(other, col)]
    for to_row, to_col in peers:
        pl.semaphore_signal(
            barrier, inc=1, device_id={"row": to_row, "col": to_col}, device_id_type=MESH
        )
    order_into(
        pos, seg, rad, cur, slot, pair, flag, main_all.at[me], extra_all.at[me], stack
    )
    pl.semaphore_wait(barrier, len(peers))

    def copies(origin, lane, to_row, to_col):
        return [
            pltpu.make_async_remote_copy(
                src_ref=target.at[origin],
                dst_ref=target.at[origin],
                send_sem=send_sem.at[part, lane],
                recv_sem=recv_sem.at[part, origin],
                device_id={"row": to_row, "col": to_col},
                device_id_type=MESH,
            )
            for part, target in enumerate(gathered)
        ]

    sent = []

    def push(origin, to_row, to_col):
        started = copies(origin, len(sent), to_row, to_col)
        for copy in started:
            copy.start()
        sent.append(started)

    def arrive(origin):
        for copy in copies(origin, 0, other, col):
            copy.wait_recv()

    def fan_out(origin):
        for k in range(1, chips):
            push(origin, row_at(row, k), col)
        push(origin, other, col)

    for k in range(col_count - 1):
        push(me, row, nearest(k))
    fan_out(me)
    stores = []

    def store(at_row):
        block = pl.ds(at_row * col_count, col_count)
        for source, outer in ((main_all, main_out), (extra_all, extra_out)):
            copy = pltpu.make_async_copy(
                source.at[block], outer.at[block], store_sem.at[len(stores)]
            )
            copy.start()
            stores.append(copy)

    places = [nearest(k) for k in range(col_count - 1)]
    for place in places:
        origin = row * col_count + place
        arrive(origin)
        fan_out(origin)
    store(row)
    for place in [col] + places:
        for k in range(1, chips):
            origin = row_at(row, chips - k) * col_count + place
            arrive(origin)
            push(origin, other, col)
    for k in range(1, chips):
        store(row_at(row, k))
    for k in range(chips):
        for place in [col] + places:
            arrive(row_at(other, chips - k) * col_count + place)
        store(row_at(other, chips - k))
    for copy in stores:
        copy.wait()
    for started in sent:
        for copy in started:
            copy.wait_send()


def gather_all(positions, segments, radius, currents, slot_of, pair_list, near_flag):
    row_count, col_count = lax.axis_size("row"), lax.axis_size("col")
    devices = row_count * col_count
    local = positions.shape[1]
    clusters = local // CS
    lanes = col_count - 1 + col_count * (row_count - 1)
    return pl.pallas_call(
        gather_kernel,
        out_shape=(
            jax.ShapeDtypeStruct((devices, clusters, 8, CS), F32),
            jax.ShapeDtypeStruct((devices, clusters + 2, CS), F32),
        ),
        in_specs=[VMEM] * 7,
        out_specs=(HBM, HBM),
        scratch_shapes=[
            pltpu.VMEM((devices, clusters, 8, CS), F32),
            pltpu.VMEM((devices, clusters + 2, CS), F32),
            pltpu.VMEM((48, local), F32),
            pltpu.SemaphoreType.DMA((2, lanes)),
            pltpu.SemaphoreType.DMA((2, devices)),
            pltpu.SemaphoreType.DMA((2 * row_count,)),
        ],
        compiler_params=pltpu.CompilerParams(collective_id=0, has_side_effects=True),
    )(
        positions,
        segments,
        radius[None, :],
        currents,
        slot_of[None, :],
        pair_list.T,
        near_flag[None, :],
    )


def on_device(positions, segments, radius, currents, resist, slot_of, pair_list, near_flag):
    main_all, extra_all = gather_all(
        positions, segments, radius, currents, slot_of, pair_list, near_flag
    )
    return pair_terms(main_all, extra_all, resist, currents, slot_of)


def solution(mesh):
    return jax.shard_map(
        on_device,
        mesh=mesh,
        in_specs=(
            P(None, ("row", "col")),
            P(None, ("row", "col")),
            P(("row", "col")),
            P(None, ("row", "col")),
            P(("row", "col")),
            P(("row", "col")),
            P(("row", "col"), None),
            P(("row", "col")),
        ),
        out_specs=P(None, ("row", "col")),
        check_vma=False,
    )
```
